32 devices in a mesh: ctx: 4 (over y, x), batch: 8 (over z, core).
Axes of the slice: x: 2, y: 2, z: 4, core: 2. Of those that a mesh axis runs over, the one named last changes fastest.
Arguments:
- tokens: bfloat16 [8, 512, 2048], P('batch', 'ctx'), may hold values from -6 to 6
- segments: int32 [8, 512], P('batch', 'ctx'), may hold values from 0 to 2, never falling along the last dimension, each value on 1 to 384 neighbouring positions
- cotangent: bfloat16 [8, 512, 2048], P('batch', 'ctx'), may hold values from -6 to 6
- attn_gain: bfloat16 [2048], P(('ctx', 'batch')), may hold values from 0.5 to 1.5
- rank_down: bfloat16 [2048, 1024], P(('ctx', 'batch')), may hold values from -0.125 to 0.125
- rank_gain: bfloat16 [1024], P(('ctx', 'batch')), may hold values from 0.5 to 1.5
- rank_up: bfloat16 [1024, 4096], P(('ctx', 'batch')), may hold values from -0.1875 to 0.1875
- key_weight: bfloat16 [2048, 256], P(('ctx', 'batch')), may hold values from -0.1875 to 0.1875
- value_weight: bfloat16 [2048, 256], P(('ctx', 'batch')), may hold values from -0.125 to 0.125
- out_weight: bfloat16 [4096, 2048], P(('ctx', 'batch')), may hold values from -1.5 to 1.5
- ffn_gain: bfloat16 [2048], P(('ctx', 'batch')), may hold values from 0.5 to 1.5
- gate_weight: bfloat16 [2048, 5632], P(('ctx', 'batch')), may hold values from -0.125 to 0.125
- up_weight: bfloat16 [2048, 5632], P(('ctx', 'batch')), may hold values from -0.125 to 0.125
- down_weight: bfloat16 [5632, 2048], P(('ctx', 'batch')), may hold values from -0.078125 to 0.078125
Outputs:
- output: bfloat16 [8, 512, 2048], P('batch', 'ctx')
- input_grad: float32 [8, 512, 2048], P('batch', 'ctx')
- grad_attn_gain: float32 [2048], P(('ctx', 'batch'))
- grad_rank_down: float32 [2048, 1024], P(('ctx', 'batch'))
- grad_rank_gain: float32 [1024], P(('ctx', 'batch'))
- grad_rank_up: float32 [1024, 4096], P(('ctx', 'batch'))
- grad_key: float32 [2048, 256], P(('ctx', 'batch'))
- grad_value: float32 [2048, 256], P(('ctx', 'batch'))
- grad_out: float32 [4096, 2048], P(('ctx', 'batch'))
- grad_ffn_gain: float32 [2048], P(('ctx', 'batch'))
- grad_gate: float32 [2048, 5632], P(('ctx', 'batch'))
- grad_up: float32 [2048, 5632], P(('ctx', 'batch'))
- grad_down: float32 [5632, 2048], P(('ctx', 'batch'))
The draws below stay inside these ranges and needn't reach their ends.
Inputs may be any that keep to these rules, and one draw needn't show every extreme that they name: `segments`: within each group the document numbers never fall; each of the 3 documents has at least one token and one has exactly 384.
All inputs are finite; a program needn't handle non-finite values.
Results may differ from the reference program's by a relative error of at most 0.015.
Values may be sent and summed in bfloat16 or wider, within the bound.
A program may use at most 384 MiB of HBM per device.

```python
import math
import jax
import jax.numpy as jnp
import numpy as np
from jax import lax

D = 2048
R = 1024
HQ = 16
DH = 256
FF = 5632
DOCS = 3
GROUPS = 8
GROUP_TOK = 512
DOC_MOST = 384


def shard_levels(own_key, extent, cuts, least, top_value):
    loudness = 1.0
    for dim, shards_of in cuts:
        heights = jax.random.uniform(jax.random.fold_in(jax.random.fold_in(own_key, 6), dim), (shards_of,), jnp.float32, least / len(cuts), top_value / len(cuts))
        loudness = loudness * jnp.repeat(jnp.exp(heights), extent[dim] // shards_of).reshape((-1,) + (1,) * (len(extent) - 1 - dim))
    return loudness


def profile(amount, total, most, skew):
    weights = [(1 << 20) // math.isqrt(standing ** skew) + 1 for standing in range(2, amount + 1)]
    spare, given = total - most - (amount - 1), [1] * (amount - 1)
    while spare > 0:
        free = [i for i in range(amount - 1) if given[i] < most]
        pool, left = sum([weights[i] for i in free]), spare
        for i in free:
            more = min(most - given[i], max(1, left * weights[i] // pool), spare)
            given[i] = given[i] + more
            spare = spare - more
    return np.array([most] + given)


def ragged_sizes(stream_key, number_of, total, bound, slope):
    if number_of == 2:
        one = jax.random.randint(stream_key, (), max(1, total - bound), min(bound, total - 1) + 1)
        return jnp.stack([one, total - one])
    tallies = jnp.asarray(profile(number_of, total, bound, slope), jnp.int32)
    pairs = (number_of - 1) // 2
    source_of, sink = tallies[1:1 + 2 * pairs:2], tallies[2:2 + 2 * pairs:2]
    margin = jnp.minimum(source_of - 1, bound - sink)
    passed = jax.random.randint(jax.random.fold_in(stream_key, 1), (pairs,), 0, 1 << 20) % (margin + 1)
    tallies = tallies.at[1:1 + 2 * pairs:2].set(source_of - passed).at[2:2 + 2 * pairs:2].set(sink + passed)
    return tallies[jax.random.permutation(jax.random.fold_in(stream_key, 2), number_of)]


def scatter_about(own_key, shape, spread, limit, cuts=(), held_as=jnp.bfloat16):
    factor_of = shard_levels(own_key, shape, cuts, -0.22, 0.18) if cuts else 1.0
    drawn = jax.random.normal(own_key, shape, jnp.float32) * spread * factor_of
    return jnp.minimum(jnp.maximum(drawn, -limit), limit).astype(held_as)


def setup_inputs(seed: int = 0) -> dict:
    key_list = jax.random.split(jax.random.key(seed), 15)
    return {
        "tokens": scatter_about(key_list[0], (GROUPS, GROUP_TOK, D), 1.0, 6.0, ((0, 8), (1, 4))),
        "segments": jax.vmap(lambda own: jnp.searchsorted(jnp.cumsum(ragged_sizes(own, DOCS, GROUP_TOK, DOC_MOST, 0)), jnp.arange(GROUP_TOK), side="right"))(jax.random.split(key_list[1], GROUPS)).reshape((GROUPS, GROUP_TOK)).astype(jnp.int32),
        "cotangent": scatter_about(key_list[2], (GROUPS, GROUP_TOK, D), 1.0, 6.0, ((0, 8), (1, 4))),
        "attn_gain": jnp.clip(1.0 + 0.1 * jax.random.normal(key_list[3], (D,), jnp.float32), 0.5, 1.5).astype(jnp.bfloat16),
        "rank_down": scatter_about(key_list[4], (D, R), D ** -0.5, 0.125, ((0, 32),)),
        "rank_gain": jnp.clip(1.0 + 0.1 * jax.random.normal(key_list[5], (R,), jnp.float32), 0.5, 1.5).astype(jnp.bfloat16),
        "rank_up": scatter_about(key_list[6], (R, HQ * DH), R ** -0.5, 0.1875, ((0, 32),)),
        "key_weight": scatter_about(key_list[7], (D, DH), (D // 2) ** -0.5, 0.1875, ((0, 32),)),
        "value_weight": scatter_about(key_list[8], (D, DH), D ** -0.5, 0.125, ((0, 32),)),
        "out_weight": scatter_about(key_list[9], (HQ * DH, D), (max(8, HQ * DH // 256)) ** -0.5, 1.5, ((0, 32),)),
        "ffn_gain": jnp.clip(1.0 + 0.1 * jax.random.normal(key_list[10], (D,), jnp.float32), 0.5, 1.5).astype(jnp.bfloat16),
        "gate_weight": scatter_about(key_list[11], (D, FF), D ** -0.5, 0.125, ((0, 32),)),
        "up_weight": scatter_about(key_list[12], (D, FF), D ** -0.5, 0.125, ((0, 32),)),
        "down_weight": scatter_about(key_list[13], (FF, D), FF ** -0.5, 0.078125, ((0, 32),)),
    }


epsilon = 1e-05
masked_value = -1e+30
highest = lax.Precision.HIGHEST

@jax.custom_vjp
def low(v):
    return lax.optimization_barrier(v.astype(jnp.bfloat16)).astype(jnp.float32)

@jax.custom_vjp
def low_back(v):
    return v

def low_keep(v):
    return (low(v), None)

def low_pass(kept, grad):
    return (grad,)

def back_keep(v):
    return (v, None)

def back_low(kept, grad):
    return (low(grad),)
low.defvjp(low_keep, low_pass)
low_back.defvjp(back_keep, back_low)

def matmul_hi(left, right):
    return jnp.dot(left, right, precision=highest)

def rms_norm(source):
    return source * lax.rsqrt(lax.optimization_barrier(jnp.mean(source * source, axis=-1, keepdims=True)) + epsilon)

def rotary_tables(positions, head_size):
    half_size = head_size // 2
    frequency = 10000.0 ** (-jnp.arange(half_size, dtype=jnp.float32) * 2.0 / head_size)
    angles = positions.astype(jnp.float32)[:, None] * frequency[None, :]
    return (jnp.cos(angles), jnp.sin(angles))

def rotary(values, cosine, sine_part):
    half_size = values.shape[-1] // 2
    front_half = values[..., :half_size]
    back_half = values[..., half_size:]
    return jnp.concatenate([front_half * cosine - back_half * sine_part, back_half * cosine + front_half * sine_part], axis=-1)

def layout(segment_row):
    index_row = jnp.arange(segment_row.shape[0], dtype=jnp.int32)
    earlier = lax.optimization_barrier(jnp.sum((segment_row[None, :] < segment_row[:, None]).astype(jnp.int32), axis=1))
    allowed = (segment_row[None, :] == segment_row[:, None]) & (index_row[None, :] <= index_row[:, None])
    return (index_row - earlier, allowed)

def group_forward(params, token_values, positions, allowed):
    whole_attn_gain, whole_rank_down, whole_rank_gain, whole_rank_up, whole_key, whole_value, whole_out, whole_ffn_gain, whole_gate, whole_up, whole_down = params
    row_count = token_values.shape[0]
    cosine, sine_part = rotary_tables(positions, DH)
    normed = low(rms_norm(token_values) * whole_attn_gain)
    rank_pre = low_back(matmul_hi(normed, whole_rank_down))
    rank_normed = low(rms_norm(rank_pre) * whole_rank_gain)
    query_pre = low_back(matmul_hi(rank_normed, whole_rank_up))
    query_heads = query_pre.reshape(row_count, HQ, DH).transpose(1, 0, 2)
    queries = low(rotary(query_heads, cosine, sine_part) * DH ** (-0.5))
    keys_all = low(rotary(low_back(matmul_hi(normed, whole_key)), cosine, sine_part))
    values_all = low(low_back(matmul_hi(normed, whole_value)))

    def one_head(query_head):
        scores = jnp.where(allowed, low_back(matmul_hi(query_head, keys_all.T)), masked_value)
        row_peak = lax.optimization_barrier(jnp.max(scores, axis=-1, keepdims=True))
        exponents = jnp.exp(scores - row_peak)
        softmax_low = low(exponents / lax.optimization_barrier(jnp.sum(exponents, axis=-1, keepdims=True)))
        return low_back(low(matmul_hi(softmax_low, values_all)))
    attended = lax.map(jax.checkpoint(one_head), queries)
    mixed = attended.transpose(1, 0, 2).reshape(row_count, HQ * DH)
    middle = token_values + low_back(matmul_hi(mixed, whole_out))
    normed_ffn = low(rms_norm(middle) * whole_ffn_gain)
    gate_pre = low_back(matmul_hi(normed_ffn, whole_gate))
    up_pre = low_back(matmul_hi(normed_ffn, whole_up))
    hidden = low(jax.nn.silu(gate_pre) * up_pre)
    return middle + low_back(matmul_hi(hidden, whole_down))

def reference(tokens, segments, cotangent, attn_gain, rank_down, rank_gain, rank_up, key_weight, value_weight, out_weight, ffn_gain, gate_weight, up_weight, down_weight):
    params = tuple((tensor.astype(jnp.float32) for tensor in (attn_gain, rank_down, rank_gain, rank_up, key_weight, value_weight, out_weight, ffn_gain, gate_weight, up_weight, down_weight)))

    def one_group(totals, group):
        group_tokens, group_segments, group_cotangent = group
        positions, allowed = layout(group_segments)

        def forward(params_in, tokens_in):
            return group_forward(params_in, tokens_in, positions, allowed)
        result, pullback = jax.vjp(forward, params, group_tokens.astype(jnp.float32))
        param_grads, token_grads = pullback(group_cotangent.astype(jnp.float32))
        totals = tuple((running + addend for running, addend in zip(totals, param_grads)))
        return (totals, (result.astype(jnp.bfloat16), token_grads))
    starting = tuple((jnp.zeros_like(tensor) for tensor in params))
    totals, (output, input_grad) = lax.scan(one_group, starting, (tokens, segments, cotangent))
    return (output, input_grad, totals[0], totals[1], totals[2], totals[3], totals[4], totals[5], totals[6], totals[7], totals[8], totals[9], totals[10])
```

```python
import jax
import jax.numpy as jnp
from jax import lax
from jax.sharding import PartitionSpec as P

epsilon = 1e-05
masked_value = -1e30
f32 = jnp.float32
bf16 = jnp.bfloat16
EVERY = ("ctx", "batch")


def rms_norm(source):
    return source * lax.rsqrt(jnp.mean(source * source, axis=-1, keepdims=True) + epsilon)


def norm_back(source, gain, upstream):
    inverse = lax.rsqrt(jnp.mean(source * source, axis=-1, keepdims=True) + epsilon)
    unit_rows = source * inverse
    gain_grad = jnp.sum(upstream * unit_rows, axis=0)
    scaled = upstream * gain
    source_grad = inverse * (
        scaled - unit_rows * jnp.mean(scaled * unit_rows, axis=-1, keepdims=True)
    )
    return (source_grad, gain_grad)


def rotary_tables(positions, head_size):
    half_size = head_size // 2
    frequency = 10000.0 ** (-jnp.arange(half_size, dtype=f32) * 2.0 / head_size)
    angles = positions.astype(f32)[:, None] * frequency[None, :]
    return (jnp.cos(angles), jnp.sin(angles))


def rotary(values, cosine, sine_part):
    half_size = values.shape[-1] // 2
    front_half = values[..., :half_size]
    back_half = values[..., half_size:]
    return jnp.concatenate(
        [front_half * cosine - back_half * sine_part, back_half * cosine + front_half * sine_part],
        axis=-1,
    )


def rotary_back(grads, cosine, sine_part):
    return rotary(grads, cosine, -sine_part)


def dot(left, right, contract):
    return lax.dot_general(
        left, right, (((contract[0],), (contract[1],)), ((), ())), preferred_element_type=f32
    )


def gather(value, axes):
    return lax.all_gather(value, axes, axis=0, tiled=True)


def scatter_sum(value, axes):
    return lax.psum_scatter(value, axes, scatter_dimension=0, tiled=True)


def shards(
    tokens,
    segments,
    cotangent,
    attn_gain,
    rank_down,
    rank_gain,
    rank_up,
    key_weight,
    value_weight,
    out_weight,
    ffn_gain,
    gate_weight,
    up_weight,
    down_weight,
):
    n_ctx, n_batch = lax.axis_size("ctx"), lax.axis_size("batch")
    ctx_rank, batch_rank = lax.axis_index("ctx"), lax.axis_index("batch")
    tok, width = tokens.shape[1:]
    group_len = n_ctx * tok
    head_size = key_weight.shape[1]
    own_cols = rank_up.shape[1] // n_ctx
    own_heads = own_cols // head_size
    rank = rank_down.shape[1]
    score_scale = head_size ** (-0.5)
    a_len, r_len, f_len = attn_gain.shape[0], rank_gain.shape[0], ffn_gain.shape[0]

    small = jnp.concatenate([attn_gain, rank_gain, ffn_gain, segments[0].astype(bf16)])
    smalls = gather(small[None], EVERY)
    whole_attn_gain = smalls[:, :a_len].reshape(-1).astype(f32)
    whole_rank_gain = smalls[:, a_len : a_len + r_len].reshape(-1).astype(f32)
    whole_ffn_gain = smalls[:, a_len + r_len : a_len + r_len + f_len].reshape(-1).astype(f32)
    group_segments = lax.dynamic_index_in_dim(
        smalls.reshape(n_ctx, n_batch, -1)[:, :, a_len + r_len + f_len :], batch_rank, 1, False
    ).reshape(-1)
    index = jnp.arange(group_len, dtype=jnp.int32)
    earlier = jnp.sum((group_segments[None, :] < group_segments[:, None]).astype(jnp.int32), axis=1)
    allowed = (group_segments[None, :] == group_segments[:, None]) & (
        index[None, :] <= index[:, None]
    )
    cosine, sine_part = rotary_tables(index - earlier, head_size)
    own_cosine = lax.dynamic_slice_in_dim(cosine, ctx_rank * tok, tok, 0)
    own_sine = lax.dynamic_slice_in_dim(sine_part, ctx_rank * tok, tok, 0)

    down_and_kv = gather(jnp.concatenate([rank_down, key_weight, value_weight], axis=1), EVERY)
    token_values = tokens[0].astype(f32)
    normed = (rms_norm(token_values) * whole_attn_gain).astype(bf16)
    pre = dot(normed, down_and_kv, (1, 0))
    rank_pre = pre[:, :rank]
    rank_normed = (rms_norm(rank_pre) * whole_rank_gain).astype(bf16)
    key_local = rotary(pre[:, rank : rank + head_size], own_cosine, own_sine).astype(bf16)
    value_local = pre[:, rank + head_size :].astype(bf16)
    joined = gather(jnp.concatenate([rank_normed, key_local, value_local], axis=1), "ctx")
    group_rank = joined[:, :rank]
    keys = joined[:, rank : rank + head_size]
    values = joined[:, rank + head_size :]

    rank_rows = rank_up.shape[0]
    up_part = lax.all_to_all(
        rank_up.reshape(rank_rows, n_ctx, own_cols).transpose(1, 0, 2), "ctx", 0, 0, tiled=True
    )
    own_rank_up = (
        lax.all_gather(up_part, "batch", axis=0)
        .transpose(1, 0, 2, 3)
        .reshape(rank, own_cols)
    )
    own_out = gather(out_weight, "batch")

    query_pre = dot(group_rank, own_rank_up, (1, 0))
    query_heads = query_pre.reshape(group_len, own_heads, head_size)
    queries = (
        (rotary(query_heads, cosine[:, None, :], sine_part[:, None, :]) * score_scale)
        .astype(bf16)
        .transpose(1, 0, 2)
    )
    scores = jnp.einsum("hqd,kd->hqk", queries, keys, preferred_element_type=f32)
    scores = jnp.where(allowed[None], scores, masked_value)
    row_peak = jnp.max(scores, axis=-1, keepdims=True)
    exponents = jnp.exp(scores - row_peak)
    probs = exponents / jnp.sum(exponents, axis=-1, keepdims=True)
    probs_low = probs.astype(bf16)
    attended = jnp.einsum("hqk,kd->hqd", probs_low, values, preferred_element_type=f32).astype(bf16)
    mixed = attended.transpose(1, 0, 2).reshape(group_len, own_cols)
    branch = scatter_sum(dot(mixed, own_out, (1, 0)).astype(bf16), "ctx")
    middle = token_values + branch.astype(f32)

    normed_ffn = (rms_norm(middle) * whole_ffn_gain).astype(bf16)
    rows, hidden_all = gate_weight.shape
    ff_rows = down_weight.shape[0]
    own_ff = n_ctx * ff_rows

    def by_owner(weight):
        return (
            weight.reshape(rows, n_ctx, n_batch, ff_rows)
            .transpose(2, 0, 1, 3)
            .reshape(n_batch, rows, own_ff)
        )

    pair = jnp.concatenate([by_owner(gate_weight), by_owner(up_weight)], axis=2)
    pair = lax.all_to_all(pair, "batch", 0, 0, tiled=True)
    gate_up = gather(pair.reshape(n_batch * rows, 2 * own_ff), "ctx")
    own_down = gather(down_weight, "ctx")
    out_grad = cotangent[0]
    grads_in = gather(out_grad, "batch")
    normed_in = gather(normed_ffn, "batch")

    both_pre = dot(normed_in, gate_up, (1, 0))
    gate_pre, up_pre = both_pre[:, :own_ff], both_pre[:, own_ff:]
    sigmoid_gate = jax.nn.sigmoid(gate_pre)
    hidden = (gate_pre * sigmoid_gate * up_pre).astype(bf16)
    result = middle + scatter_sum(dot(hidden, own_down, (1, 0)).astype(bf16), "batch").astype(f32)
    output = result.astype(bf16)[None]

    hidden_grad = dot(grads_in, own_down, (1, 1))
    gate_grad = (
        hidden_grad * up_pre * sigmoid_gate * (1.0 + gate_pre * (1.0 - sigmoid_gate))
    ).astype(bf16)
    up_grad = (hidden_grad * gate_pre * sigmoid_gate).astype(bf16)
    both_grad = jnp.concatenate([gate_grad, up_grad], axis=1)
    ffn_normed_grad = scatter_sum(dot(both_grad, gate_up, (1, 1)).astype(bf16), "batch").astype(f32)
    ffn_source_grad, term_ffn_gain = norm_back(middle, whole_ffn_gain, ffn_normed_grad)
    middle_grad = out_grad.astype(f32) + ffn_source_grad
    branch_grad = gather(middle_grad.astype(bf16), "ctx")

    grad_down = scatter_sum(dot(hidden, grads_in, (0, 0)), "ctx")
    grad_pair = scatter_sum(dot(normed_in, both_grad, (0, 0)), "ctx")
    grad_pair = lax.all_to_all(
        grad_pair.reshape(n_batch, rows, 2 * own_ff), "batch", 0, 0, tiled=True
    )

    def to_rows(part):
        return (
            part.reshape(n_batch, rows, n_ctx, ff_rows)
            .transpose(1, 2, 0, 3)
            .reshape(rows, hidden_all)
        )

    grad_gate, grad_up = to_rows(grad_pair[:, :, :own_ff]), to_rows(grad_pair[:, :, own_ff:])

    grad_out = scatter_sum(dot(mixed, branch_grad, (0, 0)), "batch")
    mixed_grad = dot(branch_grad, own_out, (1, 1)).astype(bf16)
    head_grads = mixed_grad.reshape(group_len, own_heads, head_size).transpose(1, 0, 2)
    prob_grad = jnp.einsum("hqd,kd->hqk", head_grads, values, preferred_element_type=f32)
    row_delta = jnp.sum(probs * prob_grad, axis=-1, keepdims=True)
    score_grad = (probs * (prob_grad - row_delta)).astype(bf16)
    query_grads = jnp.einsum("hqk,kd->qhd", score_grad, keys, preferred_element_type=f32)
    key_acc = jnp.einsum("hqk,hqd->kd", score_grad, queries, preferred_element_type=f32)
    value_acc = jnp.einsum("hqk,hqd->kd", probs_low, head_grads, preferred_element_type=f32)
    query_pre_grad = (
        rotary_back(query_grads * score_scale, cosine[:, None, :], sine_part[:, None, :])
        .reshape(group_len, own_cols)
        .astype(bf16)
    )
    rank_part = dot(query_pre_grad, own_rank_up, (1, 1))
    back = scatter_sum(
        jnp.concatenate([rank_part, key_acc, value_acc], axis=1).astype(bf16), "ctx"
    ).astype(f32)
    term_rank_up = dot(group_rank, query_pre_grad, (0, 0))
    term_rank_up = (
        term_rank_up.reshape(n_ctx, n_batch, rank_rows, own_cols)
        .transpose(1, 0, 2, 3)
        .reshape(n_batch * n_ctx, rank_rows, own_cols)
    )
    grad_rank_up = (
        lax.all_to_all(scatter_sum(term_rank_up, "batch"), "ctx", 0, 0, tiled=True)
        .transpose(1, 0, 2)
        .reshape(rank_rows, n_ctx * own_cols)
    )

    rank_grad_full, term_rank_gain = norm_back(rank_pre, whole_rank_gain, back[:, :rank])
    key_pre_grad = rotary_back(back[:, rank : rank + head_size], own_cosine, own_sine)
    pre_grads = jnp.concatenate(
        [rank_grad_full, key_pre_grad, back[:, rank + head_size :]], axis=1
    ).astype(bf16)
    normed_grad = dot(pre_grads, down_and_kv, (1, 1))
    attn_source_grad, term_attn_gain = norm_back(token_values, whole_attn_gain, normed_grad)
    input_grad = (middle_grad + attn_source_grad)[None]

    normed_block = lax.all_to_all(
        normed.reshape(tok, n_ctx, width // n_ctx).transpose(1, 0, 2), "ctx", 0, 0, tiled=True
    ).reshape(group_len, width // n_ctx)
    grad_dkv = scatter_sum(dot(normed_block, gather(pre_grads, "ctx"), (0, 0)), "batch")

    pieces = n_ctx * n_batch
    gain_terms = jnp.concatenate(
        [
            term_attn_gain.reshape(pieces, -1),
            term_rank_gain.reshape(pieces, -1),
            term_ffn_gain.reshape(pieces, -1),
        ],
        axis=1,
    )
    gain_sums = scatter_sum(gain_terms, EVERY)[0]
    return (
        output,
        input_grad,
        gain_sums[:a_len],
        grad_dkv[:, :rank],
        gain_sums[a_len : a_len + r_len],
        grad_rank_up,
        grad_dkv[:, rank : rank + head_size],
        grad_dkv[:, rank + head_size :],
        grad_out,
        gain_sums[a_len + r_len :],
        grad_gate,
        grad_up,
        grad_down,
    )


def solution(mesh):
    rows = P(("ctx", "batch"), None)
    line = P(("ctx", "batch"))
    toks = P("batch", "ctx", None)
    return jax.shard_map(
        shards,
        mesh=mesh,
        in_specs=(toks, P("batch", "ctx"), toks, line, rows, line) + (rows,) * 4 + (line,) + (rows,) * 3,
        out_specs=(toks, toks, line, rows, line) + (rows,) * 4 + (line,) + (rows,) * 3,
        check_vma=False,
    )
```

```python
import jax
import jax.numpy as jnp
from jax import lax
from jax.experimental import pallas as pl
from jax.experimental.pallas import tpu as pltpu
from jax.sharding import PartitionSpec as P

epsilon = 1e-05
masked_value = -1e30
f32 = jnp.float32
bf16 = jnp.bfloat16
MESH = pl.DeviceIdType.MESH


def rms_norm(source):
    return source * lax.rsqrt(jnp.mean(source * source, axis=-1, keepdims=True) + epsilon)


def norm_back(source, gain, upstream):
    inverse = lax.rsqrt(jnp.mean(source * source, axis=-1, keepdims=True) + epsilon)
    unit_rows = source * inverse
    gain_grad = jnp.sum(upstream * unit_rows, axis=0)
    scaled = upstream * gain
    source_grad = inverse * (
        scaled - unit_rows * jnp.mean(scaled * unit_rows, axis=-1, keepdims=True)
    )
    return (source_grad, gain_grad)


def rotary_tables(positions, head_size):
    half_size = head_size // 2
    frequency = 10000.0 ** (-jnp.arange(half_size, dtype=f32) * 2.0 / head_size)
    angles = positions.astype(f32)[:, None] * frequency[None, :]
    return (jnp.cos(angles), jnp.sin(angles))


def rotary(values, cosine, sine_part):
    half_size = values.shape[-1] // 2
    front_half = values[..., :half_size]
    back_half = values[..., half_size:]
    return jnp.concatenate(
        [front_half * cosine - back_half * sine_part, back_half * cosine + front_half * sine_part],
        axis=-1,
    )


def rotary_back(grads, cosine, sine_part):
    return rotary(grads, cosine, -sine_part)


def dot(left, right, contract):
    return lax.dot_general(
        left, right, (((contract[0],), (contract[1],)), ((), ())), preferred_element_type=f32
    )


def gather(value, axes):
    return lax.all_gather(value, axes, axis=0, tiled=True)


def scatter_sum(value, axes):
    return lax.psum_scatter(value, axes, scatter_dimension=0, tiled=True)


def remote(src, dst, send, recv, device):
    return pltpu.make_async_remote_copy(
        src_ref=src, dst_ref=dst, send_sem=send, recv_sem=recv, device_id=device, device_id_type=MESH
    )


class Chain:
    def __init__(self, n, own, slot, sems):
        self.m, self.own, self.slot = n // 2, own, slot
        self.s_up, self.r_up, self.s_down, self.r_down, self.s_mate, self.r_mate = sems
        self.me = lax.axis_index("batch")
        self.chip, self.core = self.me // 2, lax.rem(self.me, 2)
        self.mate = self.me + 1 - 2 * self.core

    @staticmethod
    def scratch(n):
        dma = pltpu.SemaphoreType.DMA
        return [dma((n // 2,))] * 4 + [dma((n,))] * 2

    def move(self, up, step):
        block = 2 * (self.chip - step if up else self.chip + step) + self.core
        send, recv = (self.s_up, self.r_up) if up else (self.s_down, self.r_down)
        target = self.me + 2 if up else self.me - 2
        source = self.slot(block) if step else self.own
        return remote(source, self.slot(block), send.at[step], recv.at[step], {"batch": target})

    def landed(self, up, step):
        block = 2 * (self.chip - 1 - step if up else self.chip + 1 + step) + self.core
        send, recv = (self.s_up, self.r_up) if up else (self.s_down, self.r_down)
        return block, remote(
            self.own, self.slot(block), send.at[step], recv.at[step], {"batch": self.mate}
        )

    def to_mate(self, block, k, source=None):
        place = self.slot(block)
        return remote(
            place if source is None else source,
            place,
            self.s_mate.at[k],
            self.r_mate.at[k],
            {"batch": self.mate},
        )

    def begin(self, step):
        @pl.when((self.chip < self.m - 1) & (self.chip >= step))
        def _():
            self.move(True, step).start()

        @pl.when((self.chip > 0) & (self.chip + step <= self.m - 1))
        def _():
            self.move(False, step).start()

        if step == 0:
            self.to_mate(self.me, 0, self.own).start()

    def relay(self, step):
        for up, there, k in (
            (True, self.chip - 1 - step >= 0, 1 + step),
            (False, self.chip + 1 + step <= self.m - 1, self.m + step),
        ):

            @pl.when(there)
            def _(up=up, k=k):
                block, copy = self.landed(up, step)
                copy.wait_recv()
                self.to_mate(block, k).start()

    def end(self):
        self.to_mate(self.me, 0, self.own).wait_send()
        self.to_mate(self.mate, 0, self.own).wait_recv()
        for step in range(self.m - 1):

            @pl.when((self.chip < self.m - 1) & (self.chip >= step))
            def _(step=step):
                self.move(True, step).wait_send()

            @pl.when((self.chip > 0) & (self.chip + step <= self.m - 1))
            def _(step=step):
                self.move(False, step).wait_send()

            for there, chip, k in (
                (self.chip - 1 - step >= 0, self.chip - 1 - step, 1 + step),
                (self.chip + 1 + step <= self.m - 1, self.chip + 1 + step, self.m + step),
            ):

                @pl.when(there)
                def _(chip=chip, k=k):
                    self.to_mate(2 * chip + self.core, k).wait_send()
                    self.to_mate(2 * chip + 1 - self.core, k).wait_recv()


def others_of(axis, n):
    me = lax.axis_index(axis)
    return me, [lax.rem(me + d, n) for d in range(1, n)]


def meet(n_ctx, n_batch, kinds):
    targets = []
    if any(kind.startswith("ctx") or kind.startswith("open") for kind in kinds):
        targets += [{"ctx": other} for other in others_of("ctx", n_ctx)[1]]
    if any(not kind.startswith("ctx") for kind in kinds):
        targets += [{"batch": other} for other in others_of("batch", n_batch)[1]]
    barrier = pltpu.get_barrier_semaphore()
    for target in targets:
        pl.semaphore_signal(barrier, inc=1, device_id=target, device_id_type=MESH)
    pl.semaphore_wait(barrier, len(targets))


class Spread:
    def __init__(self, axis, n, swap, source, target, sems):
        me, others = others_of(axis, n)
        self.copies = [
            remote(
                source.at[other] if swap else source,
                target.at[me],
                sems[0].at[d],
                sems[1].at[d],
                {axis: other},
            )
            for d, other in enumerate(others)
        ]
        self.keep = (me, swap, source, target)

    def begin(self):
        for copy in self.copies:
            copy.start()
        me, swap, source, target = self.keep
        target[pl.ds(me, 1)] = source[pl.ds(me, 1)] if swap else source[...][None]

    def end(self):
        for copy in self.copies:
            copy.wait()


class Square:
    def __init__(self, source, target, sems):
        self.source, self.target = source, target
        self.me = me = lax.axis_index("ctx")
        half = source.shape[0] // 2
        side, over, far = me + 1 - 2 * lax.rem(me, 2), me + 2 - 4 * (me // 2), 3 - me
        parts = (pl.ds(0, half), pl.ds(half, source.shape[0] - half))

        def own(part, to, k):
            return remote(
                source.at[parts[part]],
                target.at[me, parts[part]],
                sems[0].at[k],
                sems[1].at[k],
                {"ctx": to},
            )

        def passed(part, block, to, k):
            place = target.at[block, parts[part]]
            return remote(place, place, sems[0].at[k], sems[1].at[k], {"ctx": to})

        self.direct = [own(0, side, 0), own(1, over, 2), own(1, side, 1), own(0, over, 3)]
        self.wait_for = [passed(0, side, side, 0), passed(1, over, over, 2)]
        self.passing = [passed(0, side, over, 4), passed(1, over, side, 5)]
        self.last = [
            passed(1, side, side, 1),
            passed(0, over, over, 3),
            passed(0, far, over, 4),
            passed(1, far, side, 5),
        ]

    def begin(self):
        for copy in self.direct:
            copy.start()
        self.target[pl.ds(self.me, 1)] = self.source[...][None]

    def relay(self):
        for arrival, onward in zip(self.wait_for, self.passing):
            arrival.wait_recv()
            onward.start()

    def end(self):
        for copy in self.last:
            copy.wait_recv()
        for copy in self.direct + self.passing:
            copy.wait_send()


class CtxSum:
    def __init__(self, n, source, target, land, sems):
        self.me, others = others_of("ctx", n)
        self.source, self.target, self.land = source, target, land
        self.copies = [
            remote(source.at[other], land.at[d], sems[0].at[d], sems[1].at[d], {"ctx": other})
            for d, other in enumerate(others)
        ]

    def begin(self):
        for copy in self.copies:
            copy.start()

    def end(self):
        for copy in self.copies:
            copy.wait()
        total = self.source[self.me].astype(f32)
        for d in range(len(self.copies)):
            total = total + self.land[d].astype(f32)
        self.target[...] = total


class BatchSum:
    def __init__(self, n, source, target, pair, out, land, sems):
        me = lax.axis_index("batch")
        m, chip, core = n // 2, me // 2, lax.rem(me, 2)
        mate = me + 1 - 2 * core
        self.source, self.target, self.pair, self.out, self.land = source, target, pair, out, land
        self.order = [lax.rem(chip + d, m) for d in range(1, m)] + [chip]
        self.core = core
        self.near = [
            remote(source.at[2 * p + 1 - core], pair.at[k], sems[0].at[k], sems[1].at[k], {"batch": mate})
            for k, p in enumerate(self.order)
        ]
        self.far = [
            remote(out.at[k], land.at[k], sems[2].at[k], sems[3].at[k], {"batch": 2 * p + core})
            for k, p in enumerate(self.order[:-1])
        ]

    def begin(self):
        for copy in self.near:
            copy.start()

    def middle(self):
        for k, p in enumerate(self.order):
            self.near[k].wait_recv()
            total = self.source[2 * p + self.core].astype(f32) + self.pair[k].astype(f32)
            if k < len(self.far):
                self.out[k] = total.astype(self.out.dtype)
                self.far[k].start()
            else:
                self.target[...] = total

    def end(self):
        for copy in self.far:
            copy.wait_recv()
        total = self.target[...]
        for k in range(len(self.far)):
            total = total + self.land[k].astype(f32)
        self.target[...] = total
        for copy in self.near + self.far:
            copy.wait_send()


def exchange(number, n_ctx, n_batch, *parts):
    kinds = [kind for kind, _ in parts]
    arrays = [array for _, array in parts]
    dma = pltpu.SemaphoreType.DMA
    shapes, scratch, counts = [], [], []
    for kind, array in parts:
        shape, dtype = array.shape, array.dtype
        if kind == "ctx_gather":
            shapes.append(((n_ctx,) + shape, dtype))
            mine = [dma((max(n_ctx, 6),))] * 2
        elif kind == "ctx_swap":
            shapes.append((shape, dtype))
            mine = [dma((n_ctx,))] * 2
        elif kind == "ctx_sum":
            shapes.append((shape[1:], f32))
            mine = [pltpu.VMEM((n_ctx - 1,) + shape[1:], dtype)] + [dma((n_ctx,))] * 2
        elif kind == "batch_gather":
            shapes.append(((n_batch,) + shape, dtype))
            mine = Chain.scratch(n_batch)
        elif kind == "batch_swap":
            shapes.append((shape, dtype))
            mine = [dma((n_batch,))] * 2
        elif kind == "batch_sum":
            shapes.append((shape[1:], f32))
            m = n_batch // 2
            mine = [
                pltpu.VMEM((m,) + shape[1:], dtype),
                pltpu.VMEM((m - 1,) + shape[1:], dtype),
                pltpu.VMEM((m - 1,) + shape[1:], dtype),
            ] + [dma((m,))] * 4
        else:
            block = shape[1:] if kind == "open_swap" else shape
            shapes.append(((n_ctx, n_batch) + block, dtype))
            mine = [pltpu.VMEM((n_ctx,) + block, dtype)] + [dma((n_ctx,))] * 2
            mine = mine + Chain.scratch(n_batch)
        scratch += mine
        counts.append(len(mine))

    def kernel(*refs):
        ins, outs, rest = refs[: len(parts)], refs[len(parts) : 2 * len(parts)], refs[2 * len(parts) :]
        spreads, squares, chains, first, sums, late = [], [], [], [], [], []
        for kind, source, target, count in zip(kinds, ins, outs, counts):
            mine, rest = rest[:count], rest[count:]
            if kind == "ctx_gather" and n_ctx == 4:
                squares.append(Square(source, target, mine))
            elif kind in ("ctx_gather", "ctx_swap"):
                spreads.append(Spread("ctx", n_ctx, kind == "ctx_swap", source, target, mine))
            elif kind == "ctx_sum":
                spreads.append(CtxSum(n_ctx, source, target, mine[0], mine[1:]))
            elif kind == "batch_swap":
                spreads.append(Spread("batch", n_batch, True, source, target, mine))
            elif kind == "batch_gather":
                me = lax.axis_index("batch")
                chains.append(Chain(n_batch, source, lambda b, t=target: t.at[b], mine))
                late.append((False, target, me, source))
            elif kind == "batch_sum":
                sums.append(BatchSum(n_batch, source, target, mine[0], mine[1], mine[2], mine[3:]))
            else:
                me = lax.axis_index("batch")
                first.append(Spread("ctx", n_ctx, kind == "open_swap", source, mine[0], mine[1:3]))
                chains.append(Chain(n_batch, mine[0], lambda b, t=target: t.at[:, b], mine[3:]))
                late.append((True, target, me, mine[0]))
        meet(n_ctx, n_batch, kinds)
        for item in first:
            item.begin()
        for item in sums:
            item.begin()
        for item in squares + spreads:
            item.begin()
        for item in first:
            item.end()
        for item in sums:
            item.middle()
        if not chains:
            for item in squares:
                item.relay()
        for step in range(n_batch // 2 - 1 if chains else 0):
            for item in chains:
                item.begin(step)
            if step == 0:
                for opening, target, me, source in late:
                    if opening:
                        target[:, pl.ds(me, 1)] = source[...][:, None]
                    else:
                        target[pl.ds(me, 1)] = source[...][None]
                for item in squares:
                    item.relay()
            for item in chains:
                item.relay(step)
        for item in squares + spreads:
            item.end()
        for item in sums:
            item.end()
        for item in chains:
            item.end()

    vmem = pl.BlockSpec(memory_space=pltpu.VMEM)
    return pl.pallas_call(
        kernel,
        out_shape=[jax.ShapeDtypeStruct(shape, dtype) for shape, dtype in shapes],
        in_specs=[vmem] * len(parts),
        out_specs=[vmem] * len(parts),
        scratch_shapes=scratch,
        compiler_params=pltpu.CompilerParams(
            collective_id=number, has_side_effects=True, vmem_limit_bytes=60 * 1024 * 1024
        ),
        cost_estimate=pl.CostEstimate(flops=0, bytes_accessed=100_000_000, transcendentals=0),
        name="exchange" + str(number),
    )(*arrays)


def shards(
    tokens,
    segments,
    cotangent,
    attn_gain,
    rank_down,
    rank_gain,
    rank_up,
    key_weight,
    value_weight,
    out_weight,
    ffn_gain,
    gate_weight,
    up_weight,
    down_weight,
):
    n_ctx, n_batch = lax.axis_size("ctx"), lax.axis_size("batch")
    ctx_rank, batch_rank = lax.axis_index("ctx"), lax.axis_index("batch")
    tok, width = tokens.shape[1:]
    group_len = n_ctx * tok
    head_size = key_weight.shape[1]
    own_cols = rank_up.shape[1] // n_ctx
    own_heads = own_cols // head_size
    rank = rank_down.shape[1]
    score_scale = head_size ** (-0.5)
    a_len, r_len, f_len = attn_gain.shape[0], rank_gain.shape[0], ffn_gain.shape[0]

    part_rank, part_head = rank // n_ctx, head_size // n_ctx
    rows = rank_down.shape[0]
    rank_rows = rank_up.shape[0]

    small = jnp.concatenate([attn_gain, rank_gain, ffn_gain, segments[0].astype(bf16)])
    small = jnp.pad(small, (0, -small.shape[0] % 2048)).reshape(-1, 128)
    own_down_cols = jnp.concatenate(
        [
            rank_down.reshape(rows, n_ctx, part_rank),
            key_weight.reshape(rows, n_ctx, part_head),
            value_weight.reshape(rows, n_ctx, part_head),
        ],
        axis=2,
    ).transpose(1, 0, 2)
    own_dkv, own_rank_up, smalls, group_tokens = exchange(
        1,
        n_ctx,
        n_batch,
        ("open_swap", own_down_cols),
        ("open_swap", rank_up.reshape(rank_rows, n_ctx, own_cols).transpose(1, 0, 2)),
        ("open_gather", small),
        ("ctx_gather", tokens[0]),
    )
    own_dkv = own_dkv.reshape(width, -1)
    own_rank_up = own_rank_up.reshape(rank, own_cols)
    smalls = smalls.reshape(n_ctx * n_batch, -1)
    whole_attn_gain = smalls[:, :a_len].reshape(-1).astype(f32)
    whole_rank_gain = smalls[:, a_len : a_len + r_len].reshape(-1).astype(f32)
    whole_ffn_gain = smalls[:, a_len + r_len : a_len + r_len + f_len].reshape(-1).astype(f32)
    first_seg = a_len + r_len + f_len
    group_segments = lax.dynamic_index_in_dim(
        smalls.reshape(n_ctx, n_batch, -1)[:, :, first_seg : first_seg + tok], batch_rank, 1, False
    ).reshape(-1)
    index = jnp.arange(group_len, dtype=jnp.int32)
    earlier = jnp.sum((group_segments[None, :] < group_segments[:, None]).astype(jnp.int32), axis=1)
    allowed = (group_segments[None, :] == group_segments[:, None]) & (
        index[None, :] <= index[:, None]
    )
    cosine, sine_part = rotary_tables(index - earlier, head_size)

    def own_part(value):
        return lax.dynamic_slice_in_dim(value, ctx_rank * tok, tok, 0)

    own_cosine, own_sine = own_part(cosine), own_part(sine_part)
    token_values = tokens[0].astype(f32)
    normed = (
        rms_norm(group_tokens.reshape(group_len, width).astype(f32)) * whole_attn_gain
    ).astype(bf16)
    w_rows, hidden_all = gate_weight.shape
    ff_rows = down_weight.shape[0]
    own_ff = n_ctx * ff_rows

    def by_owner(weight):
        return (
            weight.reshape(w_rows, n_ctx, n_batch, ff_rows)
            .transpose(2, 0, 1, 3)
            .reshape(n_batch, w_rows, own_ff)
        )

    pre_parts, gate_part = exchange(
        2,
        n_ctx,
        n_batch,
        ("ctx_gather", dot(normed, own_dkv, (1, 0)).astype(bf16)),
        ("batch_swap", by_owner(gate_weight)),
    )

    def join(parts):
        return parts.transpose(1, 0, 2).reshape(group_len, -1)

    rank_pre = join(pre_parts[:, :, :part_rank]).astype(f32)
    group_rank = (rms_norm(rank_pre) * whole_rank_gain).astype(bf16)
    keys = rotary(
        join(pre_parts[:, :, part_rank : part_rank + part_head]).astype(f32), cosine, sine_part
    ).astype(bf16)
    values = join(pre_parts[:, :, part_rank + part_head :])
    rank_pre = own_part(rank_pre)
    own_out = gather(out_weight, "batch")

    query_pre = dot(group_rank, own_rank_up, (1, 0))
    query_heads = query_pre.reshape(group_len, own_heads, head_size)
    queries = (
        (rotary(query_heads, cosine[:, None, :], sine_part[:, None, :]) * score_scale)
        .astype(bf16)
        .transpose(1, 0, 2)
    )
    scores = jnp.einsum("hqd,kd->hqk", queries, keys, preferred_element_type=f32)
    scores = jnp.where(allowed[None], scores, masked_value)
    row_peak = jnp.max(scores, axis=-1, keepdims=True)
    exponents = jnp.exp(scores - row_peak)
    probs = exponents / jnp.sum(exponents, axis=-1, keepdims=True)
    probs_low = probs.astype(bf16)
    attended = jnp.einsum("hqk,kd->hqd", probs_low, values, preferred_element_type=f32).astype(bf16)
    mixed = attended.transpose(1, 0, 2).reshape(group_len, own_cols)
    branch, up_part = exchange(
        3,
        n_ctx,
        n_batch,
        ("ctx_sum", dot(mixed, own_out, (1, 0)).astype(bf16).reshape(n_ctx, tok, width)),
        ("batch_swap", by_owner(up_weight)),
    )
    middle = token_values + branch

    normed_ffn = (rms_norm(middle) * whole_ffn_gain).astype(bf16)
    own_down = gather(down_weight, "ctx")
    out_grad = cotangent[0]
    grads_in = gather(out_grad, "batch")
    normed_in, own_gate, own_up = exchange(
        4,
        n_ctx,
        n_batch,
        ("batch_gather", normed_ffn),
        ("ctx_gather", gate_part.reshape(n_batch * w_rows, own_ff)),
        ("ctx_gather", up_part.reshape(n_batch * w_rows, own_ff)),
    )
    normed_in = normed_in.reshape(n_batch * tok, width)
    own_gate, own_up = own_gate.reshape(width, own_ff), own_up.reshape(width, own_ff)

    gate_pre, up_pre = dot(normed_in, own_gate, (1, 0)), dot(normed_in, own_up, (1, 0))
    sigmoid_gate = jax.nn.sigmoid(gate_pre)
    hidden = (gate_pre * sigmoid_gate * up_pre).astype(bf16)
    out_part = dot(hidden, own_down, (1, 0)).astype(bf16)

    hidden_grad = dot(grads_in, own_down, (1, 1))
    gate_grad = (
        hidden_grad * up_pre * sigmoid_gate * (1.0 + gate_pre * (1.0 - sigmoid_gate))
    ).astype(bf16)
    up_grad = (hidden_grad * gate_pre * sigmoid_gate).astype(bf16)
    normed_part = (dot(gate_grad, own_gate, (1, 1)) + dot(up_grad, own_up, (1, 1))).astype(bf16)
    down_part = dot(hidden, grads_in, (0, 0))
    gate_sum, up_sum = dot(normed_in, gate_grad, (0, 0)), dot(normed_in, up_grad, (0, 0))
    normed_part, down_part, gate_sum, up_sum = lax.optimization_barrier(
        (normed_part, down_part, gate_sum, up_sum)
    )
    grad_down = scatter_sum(down_part, "ctx")
    gate_sum, up_sum = scatter_sum(gate_sum, "ctx"), scatter_sum(up_sum, "ctx")
    ffn_normed_grad = exchange(
        5, n_ctx, n_batch, ("batch_sum", normed_part.reshape(n_batch, tok, width))
    )[0]
    ffn_source_grad, term_ffn_gain = norm_back(middle, whole_ffn_gain, ffn_normed_grad)
    middle_grad = out_grad.astype(f32) + ffn_source_grad
    branch_grad, out_sum = exchange(
        6,
        n_ctx,
        n_batch,
        ("ctx_gather", middle_grad.astype(bf16)),
        ("batch_sum", out_part.reshape(n_batch, tok, width)),
    )
    branch_grad = branch_grad.reshape(group_len, width)
    output = (middle + out_sum).astype(bf16)[None]

    def to_rows(part):
        return (
            part.reshape(n_batch, w_rows, n_ctx, ff_rows)
            .transpose(1, 2, 0, 3)
            .reshape(w_rows, hidden_all)
        )

    def out_cols(first, last):
        part = dot(mixed, branch_grad[:, first:last], (0, 0))
        return part.reshape(n_batch, own_cols // n_batch, last - first)

    cuts = (0, 3 * width // 8 // 128 * 128, 11 * width // 16 // 128 * 128, width)
    mixed_grad = dot(branch_grad, own_out, (1, 1)).astype(bf16)
    head_grads = mixed_grad.reshape(group_len, own_heads, head_size).transpose(1, 0, 2)
    prob_grad = jnp.einsum("hqd,kd->hqk", head_grads, values, preferred_element_type=f32)
    row_delta = jnp.sum(probs * prob_grad, axis=-1, keepdims=True)
    score_grad = (probs * (prob_grad - row_delta)).astype(bf16)
    query_grads = jnp.einsum("hqk,kd->qhd", score_grad, keys, preferred_element_type=f32)
    key_acc = jnp.einsum("hqk,hqd->kd", score_grad, queries, preferred_element_type=f32)
    value_acc = jnp.einsum("hqk,hqd->kd", probs_low, head_grads, preferred_element_type=f32)
    query_pre_grad = (
        rotary_back(query_grads * score_scale, cosine[:, None, :], sine_part[:, None, :])
        .reshape(group_len, own_cols)
        .astype(bf16)
    )
    rank_part = dot(query_pre_grad, own_rank_up, (1, 1))
    back = jnp.concatenate([rank_part, key_acc, value_acc], axis=1).astype(bf16)
    back, grad_out_a = exchange(
        7,
        n_ctx,
        n_batch,
        ("ctx_sum", back.reshape(n_ctx, tok, -1)),
        ("batch_sum", out_cols(cuts[0], cuts[1])),
    )
    term_rank_up = dot(group_rank, query_pre_grad, (0, 0))
    term_rank_up = (
        term_rank_up.reshape(n_ctx, n_batch, rank_rows, own_cols)
        .transpose(1, 0, 2, 3)
        .reshape(n_batch, n_ctx, rank_rows, own_cols)
    )
    rank_grad_full, term_rank_gain = norm_back(rank_pre, whole_rank_gain, back[:, :rank])
    key_pre_grad = rotary_back(back[:, rank : rank + head_size], own_cosine, own_sine)
    pre_grads = jnp.concatenate(
        [rank_grad_full, key_pre_grad, back[:, rank + head_size :]], axis=1
    ).astype(bf16)
    pre_grads, grad_out_b = exchange(
        8,
        n_ctx,
        n_batch,
        ("ctx_gather", pre_grads),
        ("batch_sum", out_cols(cuts[1], cuts[2])),
    )
    pre_grads = pre_grads.reshape(group_len, -1)
    starts = (0, rank, rank + head_size)
    own_pre_grads = jnp.concatenate(
        [
            lax.dynamic_slice_in_dim(pre_grads, start + ctx_rank * size, size, 1)
            for start, size in zip(starts, (part_rank, part_head, part_head))
        ],
        axis=1,
    )
    normed_block = lax.dynamic_slice_in_dim(normed, ctx_rank * (width // n_ctx), width // n_ctx, 1)
    dkv_part = dot(normed_block, pre_grads, (0, 0))
    normed_grad, grad_out_c, rank_up_sum = exchange(
        9,
        n_ctx,
        n_batch,
        ("ctx_sum", dot(own_pre_grads, own_dkv, (1, 1)).astype(bf16).reshape(n_ctx, tok, width)),
        ("batch_sum", out_cols(cuts[2], cuts[3])),
        ("batch_sum", term_rank_up),
    )
    grad_out = jnp.concatenate([grad_out_a, grad_out_b, grad_out_c], axis=1)
    attn_source_grad, term_attn_gain = norm_back(token_values, whole_attn_gain, normed_grad)
    input_grad = (middle_grad + attn_source_grad)[None]

    gain_terms = jnp.concatenate(
        [
            term.reshape(n_ctx, n_batch, -1)
            for term in (term_attn_gain, term_rank_gain, term_ffn_gain)
        ],
        axis=2,
    )
    gain_terms, rank_up_sum, grad_dkv = exchange(
        10,
        n_ctx,
        n_batch,
        ("ctx_sum", gain_terms[:, :, None]),
        ("ctx_swap", rank_up_sum),
        ("batch_sum", dkv_part.reshape(n_batch, rows, -1)),
    )
    grad_rank_up = rank_up_sum.transpose(1, 0, 2).reshape(rank_rows, n_ctx * own_cols)
    gain_sums, gate_sum, up_sum = exchange(
        11,
        n_ctx,
        n_batch,
        ("batch_sum", gain_terms),
        ("batch_swap", gate_sum.reshape(n_batch, w_rows, own_ff)),
        ("batch_swap", up_sum.reshape(n_batch, w_rows, own_ff)),
    )
    gain_sums = gain_sums[0]
    grad_gate, grad_up = to_rows(gate_sum), to_rows(up_sum)
    return (
        output,
        input_grad,
        gain_sums[:a_len],
        grad_dkv[:, :rank],
        gain_sums[a_len : a_len + r_len],
        grad_rank_up,
        grad_dkv[:, rank : rank + head_size],
        grad_dkv[:, rank + head_size :],
        grad_out,
        gain_sums[a_len + r_len :],
        grad_gate,
        grad_up,
        grad_down,
    )


def solution(mesh):
    rows = P(("ctx", "batch"), None)
    line = P(("ctx", "batch"))
    toks = P("batch", "ctx", None)
    return jax.shard_map(
        shards,
        mesh=mesh,
        in_specs=(toks, P("batch", "ctx"), toks, line, rows, line) + (rows,) * 4 + (line,) + (rows,) * 3,
        out_specs=(toks, toks, line, rows, line) + (rows,) * 4 + (line,) + (rows,) * 3,
        check_vma=False,
    )
```
